512 devices in a mesh: grp: 16 (over z), blk: 32 (over x, y, core).
Axes of the slice: x: 4, y: 4, z: 16, core: 2. Of those that a mesh axis runs over, the one named last changes fastest.
Arguments:
- ancestor_inv: float32 [16, 6144, 3072], P('grp', 'blk'), as said below
- lower_block: float32 [16, 3840, 768], P('grp', 'blk'), may hold values from -0.009765625 to 0.009765625
- diag_inverse: float32 [16, 768, 768], P('grp', 'blk'), as said below
- row_index: int32 [16, 3840], P('grp'), may hold values from 0 to 6143, as said below
Outputs:
- sigma_rows: float32 [16, 3840, 768], P('grp', 'blk')
- sigma_diag: float32 [16, 768, 768], P('grp', 'blk')
The draws below stay inside these ranges and needn't reach their ends.
Inputs may be any that keep to these rules, and one draw needn't show every extreme that they name: `row_index`: for each child front: sorted increasing and distinct; exactly 120 entries fall in each aligned block of 192 consecutive indices, among them the block's first and last index. `diag_inverse`: lower triangular with a positive diagonal. `ancestor_inv`: each parent matrix assembled from its two column halves is symmetric.
All inputs are finite; a program needn't handle non-finite values.
Results may differ from the reference program's by a relative error of at most 0.0003.
Values sent between devices are 32-bit elements; how exact they have to be, the bound alone decides.
A program may use at most 64 MiB of HBM per device.

```python
import math
import jax
import jax.numpy as jnp
from jax import lax

PA = 6144
R = 3840
B = 768
CHILDREN = 16
BLOCK = 192
PICK = 120


def draw_ancestor_inv(key, part):
    parent_keys = jax.random.split(key, CHILDREN // 2)

    def one_parent(parent_key):
        key_noise, key_diag = jax.random.split(parent_key, 2)
        entries = jax.random.normal(key_noise, (PA, PA), jnp.float32)
        symmetric = (entries + entries.T) * 1.41
        row_ids = lax.broadcasted_iota(jnp.int32, (PA, PA), 0)
        col_ids = lax.broadcasted_iota(jnp.int32, (PA, PA), 1)
        diagonal = jnp.exp(jax.random.uniform(key_diag, (PA,), jnp.float32, math.log(200.0), math.log(600.0)))
        matrix = jnp.where(row_ids == col_ids, diagonal[:, None], symmetric)
        return jnp.transpose(matrix.reshape(PA, 2, PA // 2), (1, 0, 2))
    halves = lax.map(one_parent, parent_keys)
    return halves.reshape(CHILDREN, PA, PA // 2)


def draw_diag_inverse(key, part):
    key_noise, key_diag = jax.random.split(key, 2)
    shape_all = (CHILDREN, B, B)
    noise = jax.random.normal(key_noise, shape_all, jnp.float32) * 0.05
    diagonal = jnp.exp(jax.random.uniform(key_diag, shape_all, jnp.float32, math.log(0.5), math.log(2.0)))
    row_ids = lax.broadcasted_iota(jnp.int32, shape_all, 1)
    col_ids = lax.broadcasted_iota(jnp.int32, shape_all, 2)
    lower_part = jnp.where(row_ids > col_ids, noise, jnp.zeros(shape_all, jnp.float32))
    return jnp.where(row_ids == col_ids, diagonal, lower_part)


def draw_row_index(key, part):
    count_blocks = R // PICK

    def one_block(block_key, block_id):
        shuffled = jax.random.permutation(block_key, BLOCK - 2).astype(jnp.int32) + 1
        middle = jnp.sort(shuffled[:PICK - 2])
        first = jnp.zeros((1,), jnp.int32)
        last = jnp.full((1,), BLOCK - 1, jnp.int32)
        chosen = jnp.concatenate([first, middle.astype(jnp.int32), last])
        return chosen.astype(jnp.int32) + block_id * BLOCK

    def one_child(child_key):
        block_keys = jax.random.split(child_key, count_blocks)
        blocks_out = jax.vmap(one_block)(block_keys, jnp.arange(count_blocks, dtype=jnp.int32))
        return blocks_out.reshape(R).astype(jnp.int32)
    return jax.vmap(one_child)(jax.random.split(key, CHILDREN)).astype(jnp.int32)


def block_scale(key, extent, cuts, smallest, top_value):
    factor_of = 1.0
    for axis_at, blocks in cuts:
        heights = jax.random.uniform(jax.random.fold_in(jax.random.fold_in(key, 6), axis_at), (blocks,), jnp.float32, smallest / len(cuts), top_value / len(cuts))
        factor_of = factor_of * jnp.repeat(jnp.exp(heights), extent[axis_at] // blocks).reshape((-1,) + (1,) * (len(extent) - 1 - axis_at))
    return factor_of


def centred(stream_key, shape, spread, limit, shards=(), kind=jnp.bfloat16):
    result = jax.random.normal(stream_key, shape, jnp.float32) * spread
    if len(shards) > 0:
        result = block_scale(stream_key, shape, shards, -0.22, 0.18) * result
    return jnp.clip(result, min=-limit, max=limit).astype(kind)


def setup_inputs(seed: int = 0) -> dict:
    keys = jax.random.split(jax.random.key(seed), 5)
    ancestor_inv = draw_ancestor_inv(jax.random.fold_in(keys[4], 71), 0)
    lower_block = centred(keys[1], (CHILDREN, R, B), 0.00065, 0.009765625, ((0, 16), (1, 32)), jnp.float32)
    diag_inverse = draw_diag_inverse(jax.random.fold_in(keys[4], 71), 0)
    row_index = draw_row_index(jax.random.fold_in(keys[4], 71), 0)
    return dict(ancestor_inv=ancestor_inv, lower_block=lower_block, diag_inverse=diag_inverse, row_index=row_index)


def reference(ancestor_inv, lower_block, diag_inverse, row_index):
    highest = lax.Precision.HIGHEST
    count = lower_block.shape[0]

    def one_child(item):
        child, lower, pivot, names = item
        pair = lax.dynamic_slice_in_dim(ancestor_inv, (child // 2) * 2, 2, 0)
        full = jnp.concatenate([pair[0], pair[1]], axis=1)
        ancestor = jnp.take(jnp.take(full, names, axis=0), names, axis=1)
        factor = jnp.dot(lower, pivot, precision=highest, preferred_element_type=jnp.float32)
        rows_out = -jnp.dot(ancestor, factor, precision=highest, preferred_element_type=jnp.float32)
        gram = jnp.dot(pivot.T, pivot, precision=highest, preferred_element_type=jnp.float32)
        diag_out = gram - jnp.dot(factor.T, rows_out, precision=highest, preferred_element_type=jnp.float32)
        return rows_out, diag_out

    child_ids = jnp.arange(count, dtype=jnp.int32)
    sigma_rows, sigma_diag = lax.map(one_child, (child_ids, lower_block, diag_inverse, row_index))
    return sigma_rows, sigma_diag
```

```python
import jax
import jax.numpy as jnp
from jax import lax
from jax.experimental import pallas as pl
from jax.experimental.pallas import tpu as pltpu
from jax.sharding import PartitionSpec as P

MESH = pl.DeviceIdType.MESH
F32 = jnp.float32
BF16 = jnp.bfloat16
ROWS_L, ROWS_D = 120, 24
PACK = ROWS_L + ROWS_D
HALF = PACK // 2
PAD = 128


def split(v):
    hi = v.astype(BF16)
    lo = (v - hi.astype(F32)).astype(BF16)
    return hi, lo


def dot(a, b):
    return jnp.dot(a, b, preferred_element_type=F32)


def dot_t(a, b):
    return lax.dot_general(a, b, (((0,), (0,)), ((), ())), preferred_element_type=F32)


def body(tile_hbm, low_hbm, dinv_hbm, idx_hbm, rows_out, diag_out,
         tile, idx, idx_sib, picked, panel_send, panel_recv, s_hi, s_lo, packets, acc,
         d_full, part, r1_recv, r1, t1, t2, r2, t3, rows_buf,
         local_sems, send_sems, recv_sems):
    g = lax.axis_index("grp")
    b = lax.axis_index("blk")
    h = g % 2
    c = b % 2
    x = b // 8
    y = (b // 2) % 4
    pa = x * (1 - c) + y * c
    pb = y * (1 - c) + x * c
    wa = 8 - 6 * c
    wb = 2 + 6 * c

    def blk(da, db):
        return ((pa + da) % 4) * wa + ((pb + db) % 4) * wb + c

    def blk_p(da, db):
        return ((pb + da) % 4) * wb + ((pa + db) % 4) * wa + 1 - c

    def to(bb):
        return {"blk": bb}

    a_up, a_dn, b_up, b_dn, b_far = to(blk(1, 0)), to(blk(3, 0)), to(blk(0, 1)), to(blk(0, 3)), to(blk(0, 2))
    partner = to(b + 1 - 2 * c)
    sibling = {"grp": g + 1 - 2 * h}

    load_tile = pltpu.make_async_copy(tile_hbm.at[0], tile, local_sems.at[0])
    load_low = pltpu.make_async_copy(low_hbm.at[0], packets.at[b, pl.ds(0, ROWS_L)], local_sems.at[1])
    load_dinv = pltpu.make_async_copy(dinv_hbm.at[0], packets.at[b, pl.ds(ROWS_L, ROWS_D)], local_sems.at[2])
    load_idx = pltpu.make_async_copy(idx_hbm, idx, local_sems.at[3])
    load_idx.start()
    load_low.start()
    load_dinv.start()
    load_tile.start()

    barrier = pltpu.get_barrier_semaphore()
    peers = (a_up, a_dn, b_up, b_dn, b_far, partner, sibling)
    for peer in peers:
        pl.semaphore_signal(barrier, inc=1, device_id=peer, device_id_type=MESH)
    pl.semaphore_wait(barrier, len(peers))

    started = []
    names = {}

    def message(name, src, dst, device):
        m = names.setdefault(name, len(names))
        return pltpu.make_async_remote_copy(
            src_ref=src, dst_ref=dst, send_sem=send_sems.at[m], recv_sem=recv_sems.at[m],
            device_id=device, device_id_type=MESH)

    def send(name, src, dst, device):
        copy = message(name, src, dst, device)
        copy.start()
        started.append(copy)

    def receive(name, dst, device):
        message(name, dst, dst, device).wait_recv()

    def slot(k, half=None):
        if half is None:
            return packets.at[k]
        return packets.at[k, pl.ds(half * HALF, HALF)]

    load_idx.wait()
    send("idx", idx, idx_sib, sibling)
    load_low.wait()
    load_dinv.wait()

    def send_b(da):
        k = blk(da, 0)
        send(("b+", da), slot(k), slot(k), b_up)
        send(("b-", da), slot(k), slot(k), b_dn)

    def hand_over(da, db):
        k = blk(da, db)
        send(("p", da, db), slot(k), slot(k), partner)

    def take_over(da, db):
        receive(("p", da, db), slot(blk_p(da, db)), partner)

    send("a+", slot(b), slot(b), a_up)
    send("a-", slot(b), slot(b), a_dn)
    send_b(0)
    hand_over(0, 0)

    load_tile.wait()

    def pick(idx_ref, store):
        names_here = idx_ref[pl.ds(b // 2, 1), :]
        even, odd = names_here[:, :PAD], names_here[:, PAD:]
        rows_here = even * (1 - c) + odd * c
        row_ids = lax.broadcasted_iota(jnp.int32, (192, PAD), 0) + 192 * b
        row_hot = jnp.where(row_ids == rows_here, 1.0, 0.0).astype(BF16)
        for q in range(4):
            hi, lo = split(tile[:, q * 768:(q + 1) * 768])
            picked[:PAD, q * 768:(q + 1) * 768] = dot_t(row_hot, hi).astype(BF16)
            picked[PAD:, q * 768:(q + 1) * 768] = dot_t(row_hot, lo).astype(BF16)

        col_ids = lax.broadcasted_iota(jnp.int32, (384, 2 * PAD), 0)
        for p in range(8):
            cols = idx_ref[pl.ds(8 * h + p, 1), :]
            col_hot = jnp.where(col_ids + 384 * (8 * h + p) == cols, 1.0, 0.0).astype(BF16)
            both = dot(picked[:, p * 384:(p + 1) * 384], col_hot)
            store(p, both[:PAD], both[PAD:])

    def store_send(p, hi, lo):
        panel_send[p] = (hi + lo)[:ROWS_L]
        send(("s", p), panel_send.at[p], panel_recv.at[p], sibling)

    def store_own(p, hi, lo):
        s_hi[8 * h + p] = hi.astype(BF16)
        s_lo[8 * h + p] = lo.astype(BF16)

    receive("idx", idx_sib, sibling)
    pick(idx_sib, store_send)
    pick(idx, store_own)

    acc[...] = jnp.zeros_like(acc)
    receive("a+", slot(blk(3, 0)), a_dn)
    send("a+h", slot(blk(3, 0), 0), slot(blk(3, 0), 0), a_up)
    send_b(3)
    hand_over(3, 0)
    receive("a-", slot(blk(1, 0)), a_up)
    send("a-h", slot(blk(1, 0), 1), slot(blk(1, 0), 1), a_dn)
    send_b(1)
    hand_over(1, 0)

    def forward_b(da):
        receive(("b+", da), slot(blk(da, 3)), b_dn)
        send(("b+h", da), slot(blk(da, 3), 0), slot(blk(da, 3), 0), b_up)
        hand_over(da, 3)
        receive(("b-", da), slot(blk(da, 1)), b_up)
        send(("b-h", da), slot(blk(da, 1), 1), slot(blk(da, 1), 1), b_dn)
        hand_over(da, 1)

    def finish_b(da):
        receive(("b+h", da), slot(blk(da, 2), 0), b_dn)
        receive(("b-h", da), slot(blk(da, 2), 1), b_up)
        hand_over(da, 2)

    forward_b(0)
    receive("a+h", slot(blk(2, 0), 0), a_dn)
    receive("a-h", slot(blk(2, 0), 1), a_up)
    send_b(2)
    hand_over(2, 0)
    forward_b(3)
    forward_b(1)
    finish_b(0)

    def add_chip(dx, dy):
        i = ((pa + dx) % 4) * (wa // 2) + ((pb + dy) % 4) * (wb // 2)
        e_hi, e_lo = split(packets[2 * i, :PAD])
        o_hi, o_lo = split(packets[2 * i + 1, :PAD])
        l_hi = jnp.concatenate([e_hi, o_hi], axis=0)
        l_lo = jnp.concatenate([e_lo, o_lo], axis=0)
        a_hi, a_lo = s_hi[i], s_lo[i]
        acc[...] += dot(a_hi, l_hi) + dot(a_hi, l_lo) + dot(a_lo, l_hi)
        d_full[pl.ds(48 * i, 24)] = packets[2 * i, ROWS_L:]
        d_full[pl.ds(48 * i + 24, 24)] = packets[2 * i + 1, ROWS_L:]

    group_0_1 = [(0, 0), (3, 0), (1, 0), (0, 3), (0, 1)]
    group_2 = [(2, 0), (3, 3), (3, 1), (1, 3), (1, 1), (0, 2)]
    group_3 = [(2, 3), (2, 1), (3, 2), (1, 2)]

    for p in range(8):
        receive(("s", p), panel_recv.at[p], sibling)
        whole = jnp.concatenate([panel_recv[p], jnp.zeros((PAD - ROWS_L, 2 * PAD), F32)], axis=0)
        hi, lo = split(whole)
        s_hi[8 * (1 - h) + p] = hi
        s_lo[8 * (1 - h) + p] = lo
    for d in group_0_1:
        take_over(*d)
    for d in group_0_1:
        add_chip(*d)

    forward_b(2)
    finish_b(3)
    finish_b(1)
    for d in group_2:
        take_over(*d)
    for d in group_2:
        add_chip(*d)
    finish_b(2)
    for d in group_3:
        take_over(*d)
    for d in group_3:
        add_chip(*d)
    take_over(2, 2)
    add_chip(2, 2)

    stacked = jnp.concatenate([acc[...], packets[b, :PAD]], axis=0)
    m_hi, m_lo = split(stacked)
    d_hi, d_lo = split(d_full[...])
    product = dot(m_hi, d_hi) + dot(m_hi, d_lo) + dot(m_lo, d_hi)
    minus = product[:ROWS_L]
    rows_buf[...] = -minus
    store_rows = pltpu.make_async_copy(rows_buf, rows_out.at[0], local_sems.at[0])
    store_rows.start()
    own_d = packets[b, ROWS_L:]
    left_hi, left_lo = split(jnp.concatenate([product[PAD:PAD + ROWS_L], own_d], axis=0))
    right_hi, right_lo = split(jnp.concatenate([minus, own_d], axis=0))
    total = dot_t(left_hi, right_hi) + dot_t(left_hi, right_lo) + dot_t(left_lo, right_hi)
    part[...] = total.reshape(16, 2, ROWS_D, 768)

    send("r1", part.at[:, 1 - c], r1_recv, partner)
    receive("r1", r1_recv, partner)
    for i in range(16):
        ia = (i // 4) * (1 - c) + (i % 4) * c
        ib = (i % 4) * (1 - c) + (i // 4) * c
        r1[ia, ib] = part[i, c] + r1_recv[i]

    low, high = pl.ds(0, 2), pl.ds(2, 2)
    up, dn, far = (pa + 1) % 4, (pa + 3) % 4, (pa + 2) % 4
    send("ra+1", r1.at[far, low], t1.at[0], a_up)
    send("ra-1", r1.at[far, high], t1.at[1], a_dn)
    send("ra+2a", r1.at[up, high], t2.at[0, high], a_up)
    send("ra-2a", r1.at[dn, low], t2.at[1, low], a_dn)
    receive("ra+1", t1.at[0], a_dn)
    r1[up, low] = r1[up, low] + t1[0]
    send("ra+2b", r1.at[up, low], t2.at[0, low], a_up)
    receive("ra-1", t1.at[1], a_up)
    r1[dn, high] = r1[dn, high] + t1[1]
    send("ra-2b", r1.at[dn, high], t2.at[1, high], a_dn)
    receive("ra+2a", t2.at[0, high], a_dn)
    receive("ra-2a", t2.at[1, low], a_up)
    receive("ra+2b", t2.at[0, low], a_dn)
    receive("ra-2b", t2.at[1, high], a_up)
    r2[...] = r1[pa] + t2[0] + t2[1]
    send("rb+", r2.at[(pb + 1) % 4], t3.at[0], b_up)
    send("rb-", r2.at[(pb + 3) % 4], t3.at[1], b_dn)
    send("rb2", r2.at[(pb + 2) % 4], t3.at[2], b_far)
    receive("rb+", t3.at[0], b_dn)
    receive("rb-", t3.at[1], b_up)
    receive("rb2", t3.at[2], b_far)
    diag_out[0] = r2[pb] + t3[0] + t3[1] + t3[2]
    for copy in started:
        copy.wait_send()
    store_rows.wait()


def shards(ancestor_inv, lower_block, diag_inverse, row_index):
    names = row_index.reshape(32, ROWS_L)
    idx = jnp.pad(names, ((0, 0), (0, PAD - ROWS_L)), constant_values=-1).reshape(16, 2 * PAD)
    any_spec = pl.BlockSpec(memory_space=pl.ANY)
    vmem = pltpu.VMEM
    count = 80
    return pl.pallas_call(
        body,
        out_shape=(jax.ShapeDtypeStruct((1, ROWS_L, 768), F32), jax.ShapeDtypeStruct((1, ROWS_D, 768), F32)),
        in_specs=[any_spec] * 4,
        out_specs=(any_spec, pl.BlockSpec(memory_space=pltpu.VMEM)),
        scratch_shapes=[
            vmem((192, 3072), F32),
            vmem((16, 2 * PAD), jnp.int32),
            vmem((16, 2 * PAD), jnp.int32),
            vmem((2 * PAD, 3072), BF16),
            vmem((8, ROWS_L, 2 * PAD), F32),
            vmem((8, ROWS_L, 2 * PAD), F32),
            vmem((16, PAD, 2 * PAD), BF16),
            vmem((16, PAD, 2 * PAD), BF16),
            vmem((32, PACK, 768), F32),
            vmem((PAD, 768), F32),
            vmem((768, 768), F32),
            vmem((16, 2, ROWS_D, 768), F32),
            vmem((16, ROWS_D, 768), F32),
            vmem((4, 4, ROWS_D, 768), F32),
            vmem((2, 2, ROWS_D, 768), F32),
            vmem((2, 4, ROWS_D, 768), F32),
            vmem((4, ROWS_D, 768), F32),
            vmem((3, ROWS_D, 768), F32),
            vmem((ROWS_L, 768), F32),
            pltpu.SemaphoreType.DMA((4,)),
            pltpu.SemaphoreType.DMA((count,)),
            pltpu.SemaphoreType.DMA((count,)),
        ],
        compiler_params=pltpu.CompilerParams(
            collective_id=0, has_side_effects=True, vmem_limit_bytes=58 * 1024 * 1024),
    )(ancestor_inv, lower_block, diag_inverse, idx)


def solution(mesh):
    in_specs = (P("grp", "blk", None), P("grp", "blk", None), P("grp", "blk", None), P("grp", None))
    out_specs = (P("grp", "blk", None), P("grp", "blk", None))
    return jax.shard_map(shards, mesh=mesh, in_specs=in_specs, out_specs=out_specs, check_vma=False)
```

```python
import jax
import jax.numpy as jnp
from jax import lax
from jax.experimental import pallas as pl
from jax.experimental.pallas import tpu as pltpu
from jax.sharding import PartitionSpec as P

MESH = pl.DeviceIdType.MESH
F32 = jnp.float32
BF16 = jnp.bfloat16
ROWS_L, ROWS_D = 120, 24
PAD = 128
PAIR = 2 * PAD
W = 256


def split(v):
    hi = v.astype(BF16)
    lo = (v - hi.astype(F32)).astype(BF16)
    return hi, lo


def dot(a, b):
    return jnp.dot(a, b, preferred_element_type=F32)


def dot3(a_hi, a_lo, b_hi, b_lo):
    return dot(a_hi, b_hi) + dot(a_hi, b_lo) + dot(a_lo, b_hi)


def dot_t(a, b):
    return lax.dot_general(a, b, (((0,), (0,)), ((), ())), preferred_element_type=F32)


def body(tile_hbm, low_hbm, dinv_hbm, idx_hbm, rows_out, diag_out,
         tile, raw, raw_sib, idx, idx_sib, picked, panel_send, panel_recv, s_hi, s_lo,
         low_a, low_b, acc_a, acc_b, dbuf, d_hi, d_lo, left_hi, left_lo,
         part, r1_recv, r1, t1, t2, r2, t3, rows_buf,
         local_sems, send_sems, recv_sems):
    g = lax.axis_index("grp")
    b = lax.axis_index("blk")
    h = g % 2
    c = b % 2
    chip = b // 2
    x = b // 8
    y = chip % 4
    pa = x * (1 - c) + y * c
    pb = y * (1 - c) + x * c
    wa = 8 - 6 * c
    wb = 2 + 6 * c

    def blk(da, db):
        return ((pa + da) % 4) * wa + ((pb + db) % 4) * wb + c

    def blk_p(da, db):
        return ((pb + da) % 4) * wb + ((pa + db) % 4) * wa + 1 - c

    def chip_at(da, db):
        return blk(da, db) // 2

    def to(bb):
        return {"blk": bb}

    a_up, a_dn, b_up, b_dn, b_far = to(blk(1, 0)), to(blk(3, 0)), to(blk(0, 1)), to(blk(0, 3)), to(blk(0, 2))
    partner = to(b + 1 - 2 * c)
    sibling = {"grp": g + 1 - 2 * h}

    def low_piece(name, ref):
        def slot(k, half):
            first = ROWS_L * (k % 2)
            if half is None:
                return ref.at[k // 2, pl.ds(first, ROWS_L)]
            return ref.at[k // 2, pl.ds(first + 64 * half, 64 - 8 * half)]
        return (name, None, slot)

    def d_piece(j, first_block):
        def slot(k, half):
            if half is None:
                return dbuf.at[pl.ds(ROWS_D * k, ROWS_D), pl.ds(W * j, W)]
            return dbuf.at[pl.ds(ROWS_D * k, ROWS_D), pl.ds(W * j + W // 2 * half, W // 2)]
        return (("d", j), first_block, slot)

    pieces_d = [d_piece(0, None), d_piece(1, W // ROWS_D), d_piece(2, 2 * W // ROWS_D)]
    stream_a = pieces_d + [low_piece("a", low_a)]
    stream_b = [low_piece("b", low_b)]

    own_a = low_a.at[chip, pl.ds(ROWS_L * c, ROWS_L)]
    own_b = low_b.at[chip, pl.ds(ROWS_L * c, ROWS_L)]
    own_d = dbuf.at[pl.ds(ROWS_D * b, ROWS_D)]
    load_idx = pltpu.make_async_copy(idx_hbm, raw, local_sems.at[0])
    load_a = pltpu.make_async_copy(low_hbm.at[0, :, pl.ds(W, 2 * W)], own_a, local_sems.at[1])
    load_b = pltpu.make_async_copy(low_hbm.at[0, :, pl.ds(0, W)], own_b, local_sems.at[4])
    load_tile = pltpu.make_async_copy(tile_hbm.at[0], tile, local_sems.at[2])
    load_d = pltpu.make_async_copy(dinv_hbm.at[0], own_d, local_sems.at[3])
    load_idx.start()
    load_a.start()
    load_tile.start()
    load_b.start()
    dbuf[...] = jnp.zeros_like(dbuf)
    load_d.start()
    low_a[:, 2 * ROWS_L:, :] = jnp.zeros((16, PAIR - 2 * ROWS_L, 2 * W), F32)
    low_b[:, 2 * ROWS_L:, :] = jnp.zeros((16, PAIR - 2 * ROWS_L, W), F32)

    barrier = pltpu.get_barrier_semaphore()
    peers = (a_up, a_dn, b_up, b_dn, b_far, partner, sibling)
    for peer in peers:
        pl.semaphore_signal(barrier, inc=1, device_id=peer, device_id_type=MESH)
    pl.semaphore_wait(barrier, len(peers))

    started = []
    names = {}

    def message(name, src, dst, device):
        m = names.setdefault(name, len(names))
        return pltpu.make_async_remote_copy(
            src_ref=src, dst_ref=dst, send_sem=send_sems.at[m], recv_sem=recv_sems.at[m],
            device_id=device, device_id_type=MESH)

    def when(pred, run):
        if pred is None:
            run()
        else:
            pl.when(pred)(run)

    def send(name, src, dst, device, pred=None):
        copy = message(name, src, dst, device)
        when(pred, copy.start)
        started.append((copy, pred))

    def receive(name, dst, device, pred=None):
        when(pred, message(name, dst, dst, device).wait_recv)

    def send_all(stream, tag, k, half, device):
        for name, first, slot in stream:
            pred = None if first is None else k >= first
            send((name, tag), slot(k, half), slot(k, half), device, pred)

    def receive_all(stream, tag, k, half, device):
        for name, first, slot in stream:
            pred = None if first is None else k >= first
            receive((name, tag), slot(k, half), device, pred)

    def send_b(s, da):
        send_all(s, ("b+", da), blk(da, 0), None, b_up)
        send_all(s, ("b-", da), blk(da, 0), None, b_dn)

    def hand_over(s, da, db):
        send_all(s, ("p", da, db), blk(da, db), None, partner)

    def take_over(s, da, db):
        receive_all(s, ("p", da, db), blk_p(da, db), None, partner)

    def own(s):
        send_all(s, "a+", b, None, a_up)
        send_all(s, "a-", b, None, a_dn)
        send_b(s, 0)
        hand_over(s, 0, 0)

    def forward_b(s, da):
        receive_all(s, ("b+", da), blk(da, 3), None, b_dn)
        send_all(s, ("b+h", da), blk(da, 3), 0, b_up)
        hand_over(s, da, 3)
        receive_all(s, ("b-", da), blk(da, 1), None, b_up)
        send_all(s, ("b-h", da), blk(da, 1), 1, b_dn)
        hand_over(s, da, 1)

    def finish_b(s, da):
        receive_all(s, ("b+h", da), blk(da, 2), 0, b_dn)
        receive_all(s, ("b-h", da), blk(da, 2), 1, b_up)
        hand_over(s, da, 2)

    def group_1(s):
        receive_all(s, "a+", blk(3, 0), None, a_dn)
        send_all(s, "a+h", blk(3, 0), 0, a_up)
        send_b(s, 3)
        hand_over(s, 3, 0)
        receive_all(s, "a-", blk(1, 0), None, a_up)
        send_all(s, "a-h", blk(1, 0), 1, a_dn)
        send_b(s, 1)
        hand_over(s, 1, 0)
        forward_b(s, 0)

    def group_2(s):
        receive_all(s, "a+h", blk(2, 0), 0, a_dn)
        receive_all(s, "a-h", blk(2, 0), 1, a_up)
        send_b(s, 2)
        hand_over(s, 2, 0)
        forward_b(s, 3)
        forward_b(s, 1)
        finish_b(s, 0)

    def group_3(s):
        forward_b(s, 2)
        finish_b(s, 3)
        finish_b(s, 1)

    first_five = [(0, 0), (3, 0), (1, 0), (0, 3), (0, 1)]
    next_six = [(2, 0), (3, 3), (3, 1), (1, 3), (1, 1), (0, 2)]
    last_five = [(2, 3), (2, 1), (3, 2), (1, 2), (2, 2)]

    load_a.wait()
    load_d.wait()
    own(stream_a)
    load_idx.wait()
    send("idx", raw, raw_sib, sibling)

    def widen(raw_ref, idx_ref):
        pad = jnp.full((1, PAIR - 2 * ROWS_L), -1, jnp.int32)
        for i in range(16):
            names_i = raw_ref[:, 2 * ROWS_L * i:2 * ROWS_L * (i + 1)]
            idx_ref[i:i + 1, :] = jnp.concatenate([names_i, pad], axis=1)

    def pick(idx_ref, store):
        names_here = idx_ref[pl.ds(chip, 1), :]
        even, odd = names_here[:, :PAD], names_here[:, ROWS_L:ROWS_L + PAD]
        rows_here = even * (1 - c) + odd * c
        row_ids = lax.broadcasted_iota(jnp.int32, (192, PAD), 0) + 192 * b
        row_hot = jnp.where(row_ids == rows_here, 1.0, 0.0).astype(BF16)
        for q in range(4):
            hi, lo = split(tile[:, q * 768:(q + 1) * 768])
            picked[:PAD, q * 768:(q + 1) * 768] = dot_t(row_hot, hi).astype(BF16)
            picked[PAD:, q * 768:(q + 1) * 768] = dot_t(row_hot, lo).astype(BF16)

        col_ids = lax.broadcasted_iota(jnp.int32, (384, PAIR), 0)
        for p in range(8):
            cols = idx_ref[pl.ds(8 * h + p, 1), :]
            col_hot = jnp.where(col_ids + 384 * (8 * h + p) == cols, 1.0, 0.0).astype(BF16)
            both = dot(picked[:, p * 384:(p + 1) * 384], col_hot)
            store(p, both[:PAD], both[PAD:])

    def store_send(p, hi, lo):
        panel_send[p] = (hi + lo)[:ROWS_L]
        send(("s", p), panel_send.at[p], panel_recv.at[p], sibling)

    def store_own(p, hi, lo):
        s_hi[8 * h + p] = hi.astype(BF16)
        s_lo[8 * h + p] = lo.astype(BF16)

    load_tile.wait()
    receive("idx", raw_sib, sibling)
    widen(raw_sib, idx_sib)
    pick(idx_sib, store_send)
    widen(raw, idx)
    pick(idx, store_own)
    acc_a[...] = jnp.zeros_like(acc_a)
    acc_b[...] = jnp.zeros_like(acc_b)

    group_1(stream_a)
    load_b.wait()
    own(stream_b)
    group_2(stream_a)
    group_1(stream_b)

    def add_chips(stream, low, acc, group):
        for d in group:
            take_over(stream, *d)
        for d in group:
            i = chip_at(*d)
            l_hi, l_lo = split(low[i])
            acc[...] += dot3(s_hi[i], s_lo[i], l_hi, l_lo)

    group_3(stream_a)
    for p in range(8):
        receive(("s", p), panel_recv.at[p], sibling)
        whole = jnp.concatenate([panel_recv[p], jnp.zeros((PAD - ROWS_L, PAIR), F32)], axis=0)
        hi, lo = split(whole)
        s_hi[8 * (1 - h) + p] = hi
        s_lo[8 * (1 - h) + p] = lo
    add_chips(stream_a, low_a, acc_a, first_five)
    group_2(stream_b)
    add_chips(stream_a, low_a, acc_a, next_six)
    finish_b(stream_a, 2)
    add_chips(stream_a, low_a, acc_a, last_five)

    hi, lo = split(dbuf[...])
    d_hi[...] = hi
    d_lo[...] = lo
    fa_hi, fa_lo = split(own_a[...])
    fb_hi, fb_lo = split(own_b[...])
    factor = (dot3(fa_hi, fa_lo, d_hi[W:], d_lo[W:])
              + dot3(fb_hi, fb_lo, d_hi[:W], d_lo[:W]))
    hi, lo = split(jnp.concatenate([factor, own_d[...]], axis=0).T)
    left_hi[...] = hi
    left_lo[...] = lo
    group_3(stream_b)

    near, away = pl.ds(0, 2), pl.ds(2, 2)
    up, dn, far = (pa + 1) % 4, (pa + 3) % 4, (pa + 2) % 4

    def sum_steps(j):
        cols = slice(W * j, W * (j + 1))

        def step_0():
            first = max(W, W * j)
            m_hi, m_lo = split(acc_a[:, first - W:])
            product = dot3(m_hi, m_lo, d_hi[first:, cols], d_lo[first:, cols])
            if j == 0:
                m_hi, m_lo = split(acc_b[...])
                product += dot3(m_hi, m_lo, d_hi[:W, cols], d_lo[:W, cols])
            product = product[:ROWS_L]
            right_hi, right_lo = split(jnp.concatenate([product, own_d[:, cols]], axis=0))
            part[j] = dot3(left_hi[...], left_lo[...], right_hi, right_lo).reshape(16, 2, ROWS_D, W)
            send((j, "r1"), part.at[j, :, 1 - c], r1_recv.at[j], partner)
            rows_buf[:, cols] = -product

        def step_1():
            receive((j, "r1"), r1_recv.at[j], partner)
            for i in range(16):
                ia = (i // 4) * (1 - c) + (i % 4) * c
                ib = (i % 4) * (1 - c) + (i // 4) * c
                r1[j, ia, ib] = part[j, i, c] + r1_recv[j, i]
            send((j, "ra+1"), r1.at[j, far, near], t1.at[j, 0], a_up)
            send((j, "ra-1"), r1.at[j, far, away], t1.at[j, 1], a_dn)
            send((j, "ra+2a"), r1.at[j, up, away], t2.at[j, 0, away], a_up)
            send((j, "ra-2a"), r1.at[j, dn, near], t2.at[j, 1, near], a_dn)

        def step_2():
            receive((j, "ra+1"), t1.at[j, 0], a_dn)
            r1[j, up, near] = r1[j, up, near] + t1[j, 0]
            send((j, "ra+2b"), r1.at[j, up, near], t2.at[j, 0, near], a_up)
            receive((j, "ra-1"), t1.at[j, 1], a_up)
            r1[j, dn, away] = r1[j, dn, away] + t1[j, 1]
            send((j, "ra-2b"), r1.at[j, dn, away], t2.at[j, 1, away], a_dn)

        def step_3():
            receive((j, "ra+2a"), t2.at[j, 0, away], a_dn)
            receive((j, "ra-2a"), t2.at[j, 1, near], a_up)
            receive((j, "ra+2b"), t2.at[j, 0, near], a_dn)
            receive((j, "ra-2b"), t2.at[j, 1, away], a_up)
            r2[j] = r1[j, pa] + t2[j, 0] + t2[j, 1]
            send((j, "rb2"), r2.at[j, (pb + 2) % 4], t3.at[j, 2], b_far)
            send((j, "rb+"), r2.at[j, (pb + 1) % 4], t3.at[j, 0], b_up)
            send((j, "rb-"), r2.at[j, (pb + 3) % 4], t3.at[j, 1], b_dn)

        def step_4():
            receive((j, "rb+"), t3.at[j, 0], b_dn)
            receive((j, "rb-"), t3.at[j, 1], b_up)
            receive((j, "rb2"), t3.at[j, 2], b_far)
            diag_out[0, :, cols] = r2[j, pb] + t3[j, 0] + t3[j, 1] + t3[j, 2]

        return step_0, step_1, step_2, step_3, step_4

    sums = [sum_steps(j) for j in (2, 1, 0)]
    sums[0][0]()
    sums[1][0]()
    add_chips(stream_b, low_b, acc_b, first_five + next_six)
    sums[0][1]()
    sums[1][1]()
    finish_b(stream_b, 2)
    add_chips(stream_b, low_b, acc_b, last_five)
    sums[2][0]()
    store_rows = pltpu.make_async_copy(rows_buf, rows_out.at[0], local_sems.at[0])
    store_rows.start()
    for piece, step in ((0, 2), (1, 2), (2, 1), (0, 3), (1, 3), (2, 2), (0, 4), (2, 3), (1, 4), (2, 4)):
        sums[piece][step]()
    for copy, pred in started:
        when(pred, copy.wait_send)
    store_rows.wait()


def shards(ancestor_inv, lower_block, diag_inverse, row_index):
    any_spec = pl.BlockSpec(memory_space=pl.ANY)
    vmem = pltpu.VMEM
    count = 224
    return pl.pallas_call(
        body,
        out_shape=(jax.ShapeDtypeStruct((1, ROWS_L, 768), F32), jax.ShapeDtypeStruct((1, ROWS_D, 768), F32)),
        in_specs=[any_spec] * 4,
        out_specs=(any_spec, pl.BlockSpec(memory_space=pltpu.VMEM)),
        scratch_shapes=[
            vmem((192, 3072), F32),
            vmem((1, 3840), jnp.int32),
            vmem((1, 3840), jnp.int32),
            vmem((16, PAIR), jnp.int32),
            vmem((16, PAIR), jnp.int32),
            vmem((PAIR, 3072), BF16),
            vmem((8, ROWS_L, PAIR), F32),
            vmem((8, ROWS_L, PAIR), F32),
            vmem((16, PAD, PAIR), BF16),
            vmem((16, PAD, PAIR), BF16),
            vmem((16, PAIR, 2 * W), F32),
            vmem((16, PAIR, W), F32),
            vmem((PAD, 2 * W), F32),
            vmem((PAD, W), F32),
            vmem((768, 768), F32),
            vmem((768, 768), BF16),
            vmem((768, 768), BF16),
            vmem((768, ROWS_L + ROWS_D), BF16),
            vmem((768, ROWS_L + ROWS_D), BF16),
            vmem((3, 16, 2, ROWS_D, W), F32),
            vmem((3, 16, ROWS_D, W), F32),
            vmem((3, 4, 4, ROWS_D, W), F32),
            vmem((3, 2, 2, ROWS_D, W), F32),
            vmem((3, 2, 4, ROWS_D, W), F32),
            vmem((3, 4, ROWS_D, W), F32),
            vmem((3, 3, ROWS_D, W), F32),
            vmem((ROWS_L, 768), F32),
            pltpu.SemaphoreType.DMA((5,)),
            pltpu.SemaphoreType.DMA((count,)),
            pltpu.SemaphoreType.DMA((count,)),
        ],
        compiler_params=pltpu.CompilerParams(
            collective_id=0, has_side_effects=True, vmem_limit_bytes=58 * 1024 * 1024),
    )(ancestor_inv, lower_block, diag_inverse, row_index)


def solution(mesh):
    in_specs = (P("grp", "blk", None), P("grp", "blk", None), P("grp", "blk", None), P("grp", None))
    out_specs = (P("grp", "blk", None), P("grp", "blk", None))
    return jax.shard_map(shards, mesh=mesh, in_specs=in_specs, out_specs=out_specs, check_vma=False)
```

```python
import jax
import jax.numpy as jnp
from jax import lax
from jax.experimental import pallas as pl
from jax.experimental.pallas import tpu as pltpu
from jax.sharding import PartitionSpec as P

MESH = pl.DeviceIdType.MESH
F32 = jnp.float32
BF16 = jnp.bfloat16
ROWS_L, ROWS_D = 120, 24
PAD = 128
PAIR = 2 * PAD
W = 256


def split(v):
    hi = v.astype(BF16)
    lo = (v - hi.astype(F32)).astype(BF16)
    return hi, lo


def dot(a, b):
    return jnp.dot(a, b, preferred_element_type=F32)


def dot3(a_hi, a_lo, b_hi, b_lo):
    return dot(a_hi, b_hi) + dot(a_hi, b_lo) + dot(a_lo, b_hi)


def dot3s(a_both, b_hi, b_lo):
    n = a_both.shape[0] // 2
    first = dot(a_both, b_hi)
    return first[:n] + first[n:] + dot(a_both[:n], b_lo)


def dot_t(a, b):
    return lax.dot_general(a, b, (((0,), (0,)), ((), ())), preferred_element_type=F32)


def body(tile_hbm, low_hbm, dinv_hbm, idx_hbm, rows_out, diag_out,
         tile, raw, raw_sib, idx, idx_sib, picked, panel_send, panel_recv, s_both,
         low_a, low_b, acc_a, acc_b, dbuf, d_hi, d_lo, left_hi, left_lo,
         part, r1_recv, r1, t1, t2, r2, t3, rows_buf,
         local_sems, send_sems, recv_sems):
    g = lax.axis_index("grp")
    b = lax.axis_index("blk")
    h = g % 2
    c = b % 2
    chip = b // 2
    x = b // 8
    y = chip % 4
    pa = x * (1 - c) + y * c
    pb = y * (1 - c) + x * c
    wa = 8 - 6 * c
    wb = 2 + 6 * c

    def blk(da, db):
        return ((pa + da) % 4) * wa + ((pb + db) % 4) * wb + c

    def blk_p(da, db):
        return ((pb + da) % 4) * wb + ((pa + db) % 4) * wa + 1 - c

    def chip_at(da, db):
        return blk(da, db) // 2

    def to(bb):
        return {"blk": bb}

    a_up, a_dn, b_up, b_dn, b_far = to(blk(1, 0)), to(blk(3, 0)), to(blk(0, 1)), to(blk(0, 3)), to(blk(0, 2))
    partner = to(b + 1 - 2 * c)
    sibling = {"grp": g + 1 - 2 * h}

    def low_piece(name, ref):
        def slot(k, half):
            first = ROWS_L * (k % 2)
            if half is None:
                return ref.at[k // 2, pl.ds(first, ROWS_L)]
            return ref.at[k // 2, pl.ds(first + 64 * half, 64 - 8 * half)]
        return (name, None, slot)

    def d_piece(j, first_block):
        def slot(k, half):
            if half is None:
                return dbuf.at[j, pl.ds(ROWS_D * k, ROWS_D)]
            return dbuf.at[j, pl.ds(ROWS_D * k + 16 * half, 16 - 8 * half)]
        return (("d", j), first_block, slot)

    pieces_d = [d_piece(0, None), d_piece(1, W // ROWS_D), d_piece(2, 2 * W // ROWS_D)]
    stream_a = [low_piece("a", low_a)] + pieces_d
    stream_b = [low_piece("b", low_b)]

    own_a = low_a.at[chip, pl.ds(ROWS_L * c, ROWS_L)]
    own_b = low_b.at[chip, pl.ds(ROWS_L * c, ROWS_L)]
    own_rows = pl.ds(ROWS_D * b, ROWS_D)
    load_idx = pltpu.make_async_copy(idx_hbm, raw, local_sems.at[0])
    load_a = pltpu.make_async_copy(low_hbm.at[0, :, pl.ds(W, 2 * W)], own_a, local_sems.at[1])
    load_b = pltpu.make_async_copy(low_hbm.at[0, :, pl.ds(0, W)], own_b, local_sems.at[4])
    load_tile = pltpu.make_async_copy(tile_hbm.at[0], tile, local_sems.at[2])
    loads_d = [
        pltpu.make_async_copy(dinv_hbm.at[0, :, pl.ds(W * j, W)], dbuf.at[j, own_rows], local_sems.at[5 + j])
        for j in range(3)]
    load_idx.start()
    load_a.start()
    load_tile.start()
    load_b.start()
    dbuf[1, :W] = jnp.zeros((W, W), F32)
    dbuf[2, :2 * W] = jnp.zeros((2 * W, W), F32)
    for load in loads_d:
        load.start()

    barrier = pltpu.get_barrier_semaphore()
    peers = (a_up, a_dn, b_up, b_dn, b_far, partner, sibling)
    for peer in peers:
        pl.semaphore_signal(barrier, inc=1, device_id=peer, device_id_type=MESH)
    pl.semaphore_wait(barrier, len(peers))

    started = []
    settled = []
    names = {}

    def settle(upto):
        for copy, pred in started[len(settled):upto]:
            when(pred, copy.wait_send)
            settled.append(copy)

    def message(name, src, dst, device):
        m = names.setdefault(name, len(names))
        return pltpu.make_async_remote_copy(
            src_ref=src, dst_ref=dst, send_sem=send_sems.at[m], recv_sem=recv_sems.at[m],
            device_id=device, device_id_type=MESH)

    def when(pred, run):
        if pred is None:
            run()
        else:
            pl.when(pred)(run)

    def send(name, src, dst, device, pred=None):
        copy = message(name, src, dst, device)
        when(pred, copy.start)
        started.append((copy, pred))

    def receive(name, dst, device, pred=None):
        when(pred, message(name, dst, dst, device).wait_recv)

    def send_all(stream, tag, k, half, device):
        for name, first, slot in stream:
            pred = None if first is None else k >= first
            send((name, tag), slot(k, half), slot(k, half), device, pred)

    def receive_all(stream, tag, k, half, device):
        for name, first, slot in stream:
            pred = None if first is None else k >= first
            receive((name, tag), slot(k, half), device, pred)

    def take_over(s, da, db):
        receive_all(s, ("p", da, db), blk_p(da, db), None, partner)

    def hand_over(s, members):
        for da, db in members:
            send_all(s, ("p", da, db), blk(da, db), None, partner)

    def send_b(s, da):
        send_all(s, ("b+", da), blk(da, 0), None, b_up)
        send_all(s, ("b-", da), blk(da, 0), None, b_dn)

    def forward_b(s, da):
        receive_all(s, ("b+", da), blk(da, 3), None, b_dn)
        send_all(s, ("b+h", da), blk(da, 3), 0, b_up)
        receive_all(s, ("b-", da), blk(da, 1), None, b_up)
        send_all(s, ("b-h", da), blk(da, 1), 1, b_dn)

    def finish_b(s, da):
        receive_all(s, ("b+h", da), blk(da, 2), 0, b_dn)
        receive_all(s, ("b-h", da), blk(da, 2), 1, b_up)

    def own(stream):
        for piece in stream:
            s = [piece]
            send_all(s, "a+", b, None, a_up)
            send_all(s, "a-", b, None, a_dn)
            send_b(s, 0)
        hand_over(stream, [(0, 0)])

    def group_1(stream):
        for piece in stream:
            s = [piece]
            receive_all(s, "a+", blk(3, 0), None, a_dn)
            send_all(s, "a+h", blk(3, 0), 0, a_up)
            send_b(s, 3)
            receive_all(s, "a-", blk(1, 0), None, a_up)
            send_all(s, "a-h", blk(1, 0), 1, a_dn)
            send_b(s, 1)
            forward_b(s, 0)
        hand_over(stream, [(3, 0), (1, 0), (0, 3), (0, 1)])

    def group_2(stream):
        for piece in stream:
            s = [piece]
            receive_all(s, "a+h", blk(2, 0), 0, a_dn)
            receive_all(s, "a-h", blk(2, 0), 1, a_up)
            send_b(s, 2)
            forward_b(s, 3)
            forward_b(s, 1)
            finish_b(s, 0)
        hand_over(stream, [(2, 0), (3, 3), (3, 1), (1, 3), (1, 1), (0, 2)])

    def group_3(stream):
        for piece in stream:
            s = [piece]
            forward_b(s, 2)
            finish_b(s, 3)
            finish_b(s, 1)
        hand_over(stream, [(2, 3), (2, 1), (3, 2), (1, 2)])

    def group_4(stream):
        finish_b(stream, 2)
        hand_over(stream, [(2, 2)])

    first_five = [(0, 0), (3, 0), (1, 0), (0, 3), (0, 1)]
    next_six = [(2, 0), (3, 3), (3, 1), (1, 3), (1, 1), (0, 2)]
    last_five = [(2, 3), (2, 1), (3, 2), (1, 2), (2, 2)]

    load_a.wait()
    for load in loads_d:
        load.wait()
    own(stream_a)
    load_idx.wait()
    send("idx", raw, raw_sib, sibling)

    def widen(raw_ref, idx_ref):
        pad = jnp.full((1, PAIR - 2 * ROWS_L), -1, jnp.int32)
        for i in range(16):
            names_i = raw_ref[:, 2 * ROWS_L * i:2 * ROWS_L * (i + 1)]
            idx_ref[i:i + 1, :] = jnp.concatenate([names_i, pad], axis=1)

    def pick(idx_ref, store):
        names_here = idx_ref[pl.ds(chip, 1), :]
        even, odd = names_here[:, :PAD], names_here[:, ROWS_L:ROWS_L + PAD]
        rows_here = even * (1 - c) + odd * c
        row_ids = lax.broadcasted_iota(jnp.int32, (192, PAD), 0) + 192 * b
        row_hot = jnp.where(row_ids == rows_here, 1.0, 0.0).astype(BF16)
        for q in range(4):
            hi, lo = split(tile[:, q * 768:(q + 1) * 768])
            picked[:PAD, q * 768:(q + 1) * 768] = dot_t(row_hot, hi).astype(BF16)
            picked[PAD:, q * 768:(q + 1) * 768] = dot_t(row_hot, lo).astype(BF16)

        col_ids = lax.broadcasted_iota(jnp.int32, (384, PAIR), 0)
        for p in range(8):
            cols = idx_ref[pl.ds(8 * h + p, 1), :]
            col_hot = jnp.where(col_ids + 384 * (8 * h + p) == cols, 1.0, 0.0).astype(BF16)
            both = dot(picked[:, p * 384:(p + 1) * 384], col_hot)
            store(p, both[:PAD], both[PAD:])

    def store_send(p, hi, lo):
        panel_send[p] = (hi + lo)[:ROWS_L]
        send(("s", p), panel_send.at[p], panel_recv.at[p], sibling)

    def store_own(p, hi, lo):
        s_both[8 * h + p, :PAD] = hi.astype(BF16)
        s_both[8 * h + p, PAD:] = lo.astype(BF16)

    load_tile.wait()
    receive("idx", raw_sib, sibling)
    widen(raw_sib, idx_sib)
    pick(idx_sib, store_send)
    widen(raw, idx)
    pick(idx, store_own)
    low_a[:, 2 * ROWS_L:, :] = jnp.zeros((16, PAIR - 2 * ROWS_L, 2 * W), F32)
    low_b[:, 2 * ROWS_L:, :] = jnp.zeros((16, PAIR - 2 * ROWS_L, W), F32)
    acc_a[...] = jnp.zeros_like(acc_a)
    acc_b[...] = jnp.zeros_like(acc_b)

    group_1(stream_a)
    load_b.wait()
    own(stream_b)
    mark_1 = len(started)
    group_2(stream_a)
    group_1(stream_b)
    mark_2 = len(started)

    def add_chips(stream, low, acc, group):
        for d in group:
            take_over(stream, *d)
        for d in group:
            i = chip_at(*d)
            l_hi, l_lo = split(low[i])
            acc[...] += dot3s(s_both[i], l_hi, l_lo)

    group_3(stream_a)
    for p in range(8):
        receive(("s", p), panel_recv.at[p], sibling)
        whole = jnp.concatenate([panel_recv[p], jnp.zeros((PAD - ROWS_L, PAIR), F32)], axis=0)
        hi, lo = split(whole)
        s_both[8 * (1 - h) + p, :PAD] = hi
        s_both[8 * (1 - h) + p, PAD:] = lo
    add_chips(stream_a, low_a, acc_a, first_five)
    group_2(stream_b)
    settle(mark_1)
    add_chips(stream_a, low_a, acc_a, next_six)
    mark_3 = len(started)
    settle(mark_2)
    group_4(stream_a)
    group_3(stream_b)
    add_chips(stream_a, low_a, acc_a, last_five)

    for j in range(3):
        hi, lo = split(dbuf[j])
        d_hi[:, W * j:W * (j + 1)] = hi
        d_lo[:, W * j:W * (j + 1)] = lo
    own_d = jnp.concatenate([dbuf[j, own_rows] for j in range(3)], axis=1)
    fa_hi, fa_lo = split(own_a[...])
    fb_hi, fb_lo = split(own_b[...])
    factor = (dot3(fa_hi, fa_lo, d_hi[W:], d_lo[W:])
              + dot3(fb_hi, fb_lo, d_hi[:W], d_lo[:W]))
    hi, lo = split(jnp.concatenate([factor, own_d], axis=0).T)
    left_hi[...] = hi
    left_lo[...] = lo

    near, away = pl.ds(0, 2), pl.ds(2, 2)
    up, dn, far = (pa + 1) % 4, (pa + 3) % 4, (pa + 2) % 4

    def sum_steps(j):
        cols = slice(W * j, W * (j + 1))

        def step_0():
            first = max(W, W * j)
            m_both = jnp.concatenate(split(acc_a[:, first - W:]), axis=0)
            product = dot3s(m_both, d_hi[first:, cols], d_lo[first:, cols])
            if j == 0:
                m_both = jnp.concatenate(split(acc_b[...]), axis=0)
                product += dot3s(m_both, d_hi[:W, cols], d_lo[:W, cols])
            product = product[:ROWS_L]
            right_hi, right_lo = split(jnp.concatenate([product, own_d[:, cols]], axis=0))
            part[j] = dot3(left_hi[...], left_lo[...], right_hi, right_lo).reshape(16, 2, ROWS_D, W)
            send((j, "r1"), part.at[j, :, 1 - c], r1_recv.at[j], partner)
            rows_buf[:, cols] = product

        def step_1():
            receive((j, "r1"), r1_recv.at[j], partner)
            for i in range(16):
                ia = (i // 4) * (1 - c) + (i % 4) * c
                ib = (i % 4) * (1 - c) + (i // 4) * c
                r1[j, ia, ib] = part[j, i, c] + r1_recv[j, i]
            send((j, "ra+1"), r1.at[j, far, near], t1.at[j, 0], a_up)
            send((j, "ra-1"), r1.at[j, far, away], t1.at[j, 1], a_dn)
            send((j, "ra+2a"), r1.at[j, up, away], t2.at[j, 0, away], a_up)
            send((j, "ra-2a"), r1.at[j, dn, near], t2.at[j, 1, near], a_dn)

        def step_2():
            receive((j, "ra+1"), t1.at[j, 0], a_dn)
            r1[j, up, near] = r1[j, up, near] + t1[j, 0]
            send((j, "ra+2b"), r1.at[j, up, near], t2.at[j, 0, near], a_up)
            receive((j, "ra-1"), t1.at[j, 1], a_up)
            r1[j, dn, away] = r1[j, dn, away] + t1[j, 1]
            send((j, "ra-2b"), r1.at[j, dn, away], t2.at[j, 1, away], a_dn)

        def step_3():
            receive((j, "ra+2a"), t2.at[j, 0, away], a_dn)
            receive((j, "ra-2a"), t2.at[j, 1, near], a_up)
            receive((j, "ra+2b"), t2.at[j, 0, near], a_dn)
            receive((j, "ra-2b"), t2.at[j, 1, away], a_up)
            r2[j] = r1[j, pa] + t2[j, 0] + t2[j, 1]
            send((j, "rb2"), r2.at[j, (pb + 2) % 4], t3.at[j, 2], b_far)
            send((j, "rb+"), r2.at[j, (pb + 1) % 4], t3.at[j, 0], b_up)
            send((j, "rb-"), r2.at[j, (pb + 3) % 4], t3.at[j, 1], b_dn)

        def step_4():
            receive((j, "rb+"), t3.at[j, 0], b_dn)
            receive((j, "rb-"), t3.at[j, 1], b_up)
            receive((j, "rb2"), t3.at[j, 2], b_far)
            diag_out[0, :, cols] = r2[j, pb] + t3[j, 0] + t3[j, 1] + t3[j, 2]

        return step_0, step_1, step_2, step_3, step_4

    sums = [sum_steps(j) for j in (2, 1, 0)]
    sums[0][0]()
    sums[1][0]()
    add_chips(stream_b, low_b, acc_b, first_five + next_six)
    sums[0][1]()
    sums[1][1]()
    settle(mark_3)
    group_4(stream_b)
    add_chips(stream_b, low_b, acc_b, last_five)
    sums[2][0]()
    store_rows = pltpu.make_async_copy(rows_buf, rows_out.at[0], local_sems.at[0])
    store_rows.start()
    for piece, step in ((0, 2), (2, 1), (1, 2), (0, 3), (2, 2), (1, 3), (0, 4), (2, 3), (1, 4), (2, 4)):
        sums[piece][step]()
    settle(len(started))
    store_rows.wait()


def negate(rows_ref, diag_ref, rows_out, diag_out):
    rows_out[...] = -rows_ref[...]
    diag_out[...] = diag_ref[...]


def shards(ancestor_inv, lower_block, diag_inverse, row_index):
    any_spec = pl.BlockSpec(memory_space=pl.ANY)
    vmem = pltpu.VMEM
    count = 224
    rows, diag = pl.pallas_call(
        body,
        out_shape=(jax.ShapeDtypeStruct((1, ROWS_L, 768), F32), jax.ShapeDtypeStruct((1, ROWS_D, 768), F32)),
        in_specs=[any_spec] * 4,
        out_specs=(any_spec, pl.BlockSpec(memory_space=pltpu.VMEM)),
        scratch_shapes=[
            vmem((192, 3072), F32),
            vmem((1, 3840), jnp.int32),
            vmem((1, 3840), jnp.int32),
            vmem((16, PAIR), jnp.int32),
            vmem((16, PAIR), jnp.int32),
            vmem((PAIR, 3072), BF16),
            vmem((8, ROWS_L, PAIR), F32),
            vmem((8, ROWS_L, PAIR), F32),
            vmem((16, 2 * PAD, PAIR), BF16),
            vmem((16, PAIR, 2 * W), F32),
            vmem((16, PAIR, W), F32),
            vmem((PAD, 2 * W), F32),
            vmem((PAD, W), F32),
            vmem((3, 768, W), F32),
            vmem((768, 768), BF16),
            vmem((768, 768), BF16),
            vmem((768, ROWS_L + ROWS_D), BF16),
            vmem((768, ROWS_L + ROWS_D), BF16),
            vmem((3, 16, 2, ROWS_D, W), F32),
            vmem((3, 16, ROWS_D, W), F32),
            vmem((3, 4, 4, ROWS_D, W), F32),
            vmem((3, 2, 2, ROWS_D, W), F32),
            vmem((3, 2, 4, ROWS_D, W), F32),
            vmem((3, 4, ROWS_D, W), F32),
            vmem((3, 3, ROWS_D, W), F32),
            vmem((ROWS_L, 768), F32),
            pltpu.SemaphoreType.DMA((8,)),
            pltpu.SemaphoreType.DMA((count,)),
            pltpu.SemaphoreType.DMA((count,)),
        ],
        compiler_params=pltpu.CompilerParams(
            collective_id=0, has_side_effects=True, vmem_limit_bytes=58 * 1024 * 1024),
    )(ancestor_inv, lower_block, diag_inverse, row_index)
    return pl.pallas_call(
        negate,
        out_shape=(jax.ShapeDtypeStruct(rows.shape, F32), jax.ShapeDtypeStruct(diag.shape, F32)),
    )(rows, diag)


def solution(mesh):
    in_specs = (P("grp", "blk", None), P("grp", "blk", None), P("grp", "blk", None), P("grp", None))
    out_specs = (P("grp", "blk", None), P("grp", "blk", None))
    return jax.shard_map(shards, mesh=mesh, in_specs=in_specs, out_specs=out_specs, check_vma=False)
```

```python
import jax
import jax.numpy as jnp
from jax import lax
from jax.experimental import pallas as pl
from jax.experimental.pallas import tpu as pltpu
from jax.sharding import PartitionSpec as P

MESH = pl.DeviceIdType.MESH
F32 = jnp.float32
BF16 = jnp.bfloat16
ROWS_L, ROWS_D = 120, 24
PAD = 128
PAIR = 2 * PAD
W = 256


def split(v):
    hi = v.astype(BF16)
    lo = (v - hi.astype(F32)).astype(BF16)
    return hi, lo


def dot(a, b):
    return jnp.dot(a, b, preferred_element_type=F32)


def dot3(a_hi, a_lo, b_hi, b_lo):
    return dot(a_hi, b_hi) + dot(a_hi, b_lo) + dot(a_lo, b_hi)


def dot3s(a_both, b_hi, b_lo):
    n = a_both.shape[0] // 2
    first = dot(a_both, b_hi)
    return first[:n] + first[n:] + dot(a_both[:n], b_lo)


def dot_t(a, b):
    return lax.dot_general(a, b, (((0,), (0,)), ((), ())), preferred_element_type=F32)


def body(tile_hbm, low_hbm, dinv_hbm, idx_hbm, rows_out, diag_out,
         tile, raw, raw_sib, idx, idx_sib, picked, panel_send, panel_recv, s_both,
         low_a, low_b, acc_a, acc_b, dbuf, d_hi, d_lo, left_hi, left_lo,
         part, r1_recv, r1, t1, t2, r2, t3, rows_buf,
         local_sems, send_sems, recv_sems):
    g = lax.axis_index("grp")
    b = lax.axis_index("blk")
    h = g % 2
    c = b % 2
    chip = b // 2
    x = b // 8
    y = chip % 4
    pa = x * (1 - c) + y * c
    pb = y * (1 - c) + x * c
    wa = 8 - 6 * c
    wb = 2 + 6 * c

    def blk(da, db):
        return ((pa + da) % 4) * wa + ((pb + db) % 4) * wb + c

    def blk_p(da, db):
        return ((pb + da) % 4) * wb + ((pa + db) % 4) * wa + 1 - c

    def chip_at(da, db):
        return blk(da, db) // 2

    def to(bb):
        return {"blk": bb}

    a_up, a_dn, b_up, b_dn, b_far = to(blk(1, 0)), to(blk(3, 0)), to(blk(0, 1)), to(blk(0, 3)), to(blk(0, 2))
    partner = to(b + 1 - 2 * c)
    sibling = {"grp": g + 1 - 2 * h}

    def low_piece(name, ref):
        def slot(k, half):
            first = ROWS_L * (k % 2)
            if half is None:
                return ref.at[k // 2, pl.ds(first, ROWS_L)]
            return ref.at[k // 2, pl.ds(first + 64 * half, 64 - 8 * half)]
        return (name, None, slot)

    def d_piece(pieces):
        size = ROWS_D * pieces
        split_at = size // 16 * 8

        def slot(k, half):
            if half is None:
                return dbuf.at[k, pl.ds(0, size)]
            return dbuf.at[k, pl.ds(half * split_at, split_at + half * (size - 2 * split_at))]

        def has(k):
            enough = k >= (0, W // ROWS_D, 2 * W // ROWS_D)[pieces - 1]
            return enough if pieces == 3 else jnp.logical_and(enough, k < (W // ROWS_D, 2 * W // ROWS_D)[pieces - 1])
        return ("d", has, slot)

    pieces_d = [d_piece(1), d_piece(2), d_piece(3)]
    stream_a = [low_piece("a", low_a)] + pieces_d
    stream_b = [low_piece("b", low_b)]

    own_a = low_a.at[chip, pl.ds(ROWS_L * c, ROWS_L)]
    own_b = low_b.at[chip, pl.ds(ROWS_L * c, ROWS_L)]
    load_idx = pltpu.make_async_copy(idx_hbm, raw, local_sems.at[0])
    load_a = pltpu.make_async_copy(low_hbm.at[0, :, pl.ds(W, 2 * W)], own_a, local_sems.at[1])
    load_b = pltpu.make_async_copy(low_hbm.at[0, :, pl.ds(0, W)], own_b, local_sems.at[4])
    load_tile = pltpu.make_async_copy(tile_hbm.at[0], tile, local_sems.at[2])
    loads_d = [
        pltpu.make_async_copy(dinv_hbm.at[0, :, pl.ds(W * j, W)], dbuf.at[b, pl.ds(ROWS_D * j, ROWS_D)], local_sems.at[5 + j])
        for j in range(3)]
    load_idx.start()
    load_a.start()
    load_tile.start()
    load_b.start()
    dbuf[:W // ROWS_D, ROWS_D:] = jnp.zeros((W // ROWS_D, 2 * ROWS_D, W), F32)
    dbuf[W // ROWS_D:2 * W // ROWS_D, 2 * ROWS_D:] = jnp.zeros((2 * W // ROWS_D - W // ROWS_D, ROWS_D, W), F32)
    for load in loads_d:
        load.start()

    barrier = pltpu.get_barrier_semaphore()
    peers = (a_up, a_dn, b_up, b_dn, b_far, partner, sibling)
    for peer in peers:
        pl.semaphore_signal(barrier, inc=1, device_id=peer, device_id_type=MESH)
    pl.semaphore_wait(barrier, len(peers))

    started = []
    settled = []
    names = {}

    def settle(upto):
        for copy, pred in started[len(settled):upto]:
            when(pred, copy.wait_send)
            settled.append(copy)

    def message(name, src, dst, device):
        m = names.setdefault(name, len(names))
        return pltpu.make_async_remote_copy(
            src_ref=src, dst_ref=dst, send_sem=send_sems.at[m], recv_sem=recv_sems.at[m],
            device_id=device, device_id_type=MESH)

    def when(pred, run):
        if pred is None:
            run()
        else:
            pl.when(pred)(run)

    def send(name, src, dst, device, pred=None):
        copy = message(name, src, dst, device)
        when(pred, copy.start)
        started.append((copy, pred))

    def receive(name, dst, device, pred=None):
        when(pred, message(name, dst, dst, device).wait_recv)

    def send_all(stream, tag, k, half, device):
        for name, first, slot in stream:
            pred = None if first is None else first(k)
            send((name, tag), slot(k, half), slot(k, half), device, pred)

    def receive_all(stream, tag, k, half, device):
        for name, first, slot in stream:
            pred = None if first is None else first(k)
            receive((name, tag), slot(k, half), device, pred)

    def take_over(s, da, db):
        receive_all(s, ("p", da, db), blk_p(da, db), None, partner)

    def hand_over(s, members):
        for da, db in members:
            send_all(s, ("p", da, db), blk(da, db), None, partner)

    def send_b(s, da):
        send_all(s, ("b+", da), blk(da, 0), None, b_up)
        send_all(s, ("b-", da), blk(da, 0), None, b_dn)

    def forward_b(s, da):
        receive_all(s, ("b+", da), blk(da, 3), None, b_dn)
        send_all(s, ("b+h", da), blk(da, 3), 0, b_up)
        receive_all(s, ("b-", da), blk(da, 1), None, b_up)
        send_all(s, ("b-h", da), blk(da, 1), 1, b_dn)

    def finish_b(s, da):
        receive_all(s, ("b+h", da), blk(da, 2), 0, b_dn)
        receive_all(s, ("b-h", da), blk(da, 2), 1, b_up)

    def own(stream):
        for piece in stream:
            s = [piece]
            send_all(s, "a+", b, None, a_up)
            send_all(s, "a-", b, None, a_dn)
            send_b(s, 0)
        hand_over(stream, [(0, 0)])

    def group_1(stream):
        for piece in stream:
            s = [piece]
            receive_all(s, "a+", blk(3, 0), None, a_dn)
            send_all(s, "a+h", blk(3, 0), 0, a_up)
            send_b(s, 3)
            receive_all(s, "a-", blk(1, 0), None, a_up)
            send_all(s, "a-h", blk(1, 0), 1, a_dn)
            send_b(s, 1)
            forward_b(s, 0)
        hand_over(stream, [(3, 0), (1, 0), (0, 3), (0, 1)])

    def group_2(stream):
        for piece in stream:
            s = [piece]
            receive_all(s, "a+h", blk(2, 0), 0, a_dn)
            receive_all(s, "a-h", blk(2, 0), 1, a_up)
            send_b(s, 2)
            forward_b(s, 3)
            forward_b(s, 1)
            finish_b(s, 0)
        hand_over(stream, [(2, 0), (3, 3), (3, 1), (1, 3), (1, 1), (0, 2)])

    def group_3(stream):
        for piece in stream:
            s = [piece]
            forward_b(s, 2)
            finish_b(s, 3)
            finish_b(s, 1)
        hand_over(stream, [(2, 3), (2, 1), (3, 2), (1, 2)])

    def group_4(stream):
        finish_b(stream, 2)
        hand_over(stream, [(2, 2)])

    first_five = [(0, 0), (3, 0), (1, 0), (0, 3), (0, 1)]
    next_six = [(2, 0), (3, 3), (3, 1), (1, 3), (1, 1), (0, 2)]
    last_five = [(2, 3), (2, 1), (3, 2), (1, 2), (2, 2)]

    load_a.wait()
    for load in loads_d:
        load.wait()
    own(stream_a)
    load_idx.wait()
    send("idx", raw, raw_sib, sibling)

    def widen(raw_ref, idx_ref):
        pad = jnp.full((1, PAIR - 2 * ROWS_L), -1, jnp.int32)
        for i in range(16):
            names_i = raw_ref[:, 2 * ROWS_L * i:2 * ROWS_L * (i + 1)]
            idx_ref[i:i + 1, :] = jnp.concatenate([names_i, pad], axis=1)

    def pick(idx_ref, store):
        names_here = idx_ref[pl.ds(chip, 1), :]
        even, odd = names_here[:, :PAD], names_here[:, ROWS_L:ROWS_L + PAD]
        rows_here = even * (1 - c) + odd * c
        row_ids = lax.broadcasted_iota(jnp.int32, (192, PAD), 0) + 192 * b
        row_hot = jnp.where(row_ids == rows_here, 1.0, 0.0).astype(BF16)
        for q in range(4):
            hi, lo = split(tile[:, q * 768:(q + 1) * 768])
            picked[:PAD, q * 768:(q + 1) * 768] = dot_t(row_hot, hi).astype(BF16)
            picked[PAD:, q * 768:(q + 1) * 768] = dot_t(row_hot, lo).astype(BF16)

        col_ids = lax.broadcasted_iota(jnp.int32, (384, PAIR), 0)
        for p in range(8):
            cols = idx_ref[pl.ds(8 * h + p, 1), :]
            col_hot = jnp.where(col_ids + 384 * (8 * h + p) == cols, 1.0, 0.0).astype(BF16)
            both = dot(picked[:, p * 384:(p + 1) * 384], col_hot)
            store(p, both[:PAD], both[PAD:])

    def store_send(p, hi, lo):
        panel_send[p] = (hi + lo)[:ROWS_L]
        send(("s", p), panel_send.at[p], panel_recv.at[p], sibling)

    def store_own(p, hi, lo):
        s_both[8 * h + p, :PAD] = hi.astype(BF16)
        s_both[8 * h + p, PAD:] = lo.astype(BF16)

    load_tile.wait()
    receive("idx", raw_sib, sibling)
    widen(raw_sib, idx_sib)
    pick(idx_sib, store_send)
    widen(raw, idx)
    pick(idx, store_own)
    low_a[:, 2 * ROWS_L:, :] = jnp.zeros((16, PAIR - 2 * ROWS_L, 2 * W), F32)
    low_b[:, 2 * ROWS_L:, :] = jnp.zeros((16, PAIR - 2 * ROWS_L, W), F32)
    acc_a[...] = jnp.zeros_like(acc_a)
    acc_b[...] = jnp.zeros_like(acc_b)

    group_1(stream_a)
    load_b.wait()
    own(stream_b)
    mark_1 = len(started)
    group_2(stream_a)
    group_1(stream_b)
    mark_2 = len(started)

    def add_chips(stream, low, acc, group):
        for d in group:
            take_over(stream, *d)
        for d in group:
            i = chip_at(*d)
            l_hi, l_lo = split(low[i])
            acc[...] += dot3s(s_both[i], l_hi, l_lo)

    group_3(stream_a)
    for p in range(8):
        receive(("s", p), panel_recv.at[p], sibling)
        whole = jnp.concatenate([panel_recv[p], jnp.zeros((PAD - ROWS_L, PAIR), F32)], axis=0)
        hi, lo = split(whole)
        s_both[8 * (1 - h) + p, :PAD] = hi
        s_both[8 * (1 - h) + p, PAD:] = lo
    add_chips(stream_a, low_a, acc_a, first_five)
    group_2(stream_b)
    settle(mark_1)
    add_chips(stream_a, low_a, acc_a, next_six)
    mark_3 = len(started)
    settle(mark_2)
    group_4(stream_a)
    group_3(stream_b)
    add_chips(stream_a, low_a, acc_a, last_five)

    for j in range(3):
        hi, lo = split(dbuf[:, ROWS_D * j:ROWS_D * (j + 1)].reshape(768, W))
        d_hi[:, W * j:W * (j + 1)] = hi
        d_lo[:, W * j:W * (j + 1)] = lo
    own_d = jnp.concatenate([dbuf[b, pl.ds(ROWS_D * j, ROWS_D)] for j in range(3)], axis=1)
    fa_hi, fa_lo = split(own_a[...])
    fb_hi, fb_lo = split(own_b[...])
    factor = (dot3(fa_hi, fa_lo, d_hi[W:], d_lo[W:])
              + dot3(fb_hi, fb_lo, d_hi[:W], d_lo[:W]))
    hi, lo = split(jnp.concatenate([factor, own_d], axis=0).T)
    left_hi[...] = hi
    left_lo[...] = lo

    near, away = pl.ds(0, 2), pl.ds(2, 2)
    up, dn, far = (pa + 1) % 4, (pa + 3) % 4, (pa + 2) % 4

    def sum_steps(j):
        cols = slice(W * j, W * (j + 1))

        def step_0():
            first = max(W, W * j)
            m_both = jnp.concatenate(split(acc_a[:, first - W:]), axis=0)
            product = dot3s(m_both, d_hi[first:, cols], d_lo[first:, cols])
            if j == 0:
                m_both = jnp.concatenate(split(acc_b[...]), axis=0)
                product += dot3s(m_both, d_hi[:W, cols], d_lo[:W, cols])
            product = product[:ROWS_L]
            right_hi, right_lo = split(jnp.concatenate([product, own_d[:, cols]], axis=0))
            part[j] = dot3(left_hi[...], left_lo[...], right_hi, right_lo).reshape(16, 2, ROWS_D, W)
            send((j, "r1"), part.at[j, :, 1 - c], r1_recv.at[j], partner)
            rows_buf[:, cols] = product

        def step_1():
            receive((j, "r1"), r1_recv.at[j], partner)
            for i in range(16):
                ia = (i // 4) * (1 - c) + (i % 4) * c
                ib = (i % 4) * (1 - c) + (i // 4) * c
                r1[j, ia, ib] = part[j, i, c] + r1_recv[j, i]
            send((j, "ra+1"), r1.at[j, far, near], t1.at[j, 0], a_up)
            send((j, "ra-1"), r1.at[j, far, away], t1.at[j, 1], a_dn)
            send((j, "ra+2a"), r1.at[j, up, away], t2.at[j, 0, away], a_up)
            send((j, "ra-2a"), r1.at[j, dn, near], t2.at[j, 1, near], a_dn)

        def step_2():
            receive((j, "ra+1"), t1.at[j, 0], a_dn)
            r1[j, up, near] = r1[j, up, near] + t1[j, 0]
            send((j, "ra+2b"), r1.at[j, up, near], t2.at[j, 0, near], a_up)
            receive((j, "ra-1"), t1.at[j, 1], a_up)
            r1[j, dn, away] = r1[j, dn, away] + t1[j, 1]
            send((j, "ra-2b"), r1.at[j, dn, away], t2.at[j, 1, away], a_dn)

        def step_3():
            receive((j, "ra+2a"), t2.at[j, 0, away], a_dn)
            receive((j, "ra-2a"), t2.at[j, 1, near], a_up)
            receive((j, "ra+2b"), t2.at[j, 0, near], a_dn)
            receive((j, "ra-2b"), t2.at[j, 1, away], a_up)
            r2[j] = r1[j, pa] + t2[j, 0] + t2[j, 1]
            send((j, "rb2"), r2.at[j, (pb + 2) % 4], t3.at[j, 2], b_far)
            send((j, "rb+"), r2.at[j, (pb + 1) % 4], t3.at[j, 0], b_up)
            send((j, "rb-"), r2.at[j, (pb + 3) % 4], t3.at[j, 1], b_dn)

        def step_4():
            receive((j, "rb+"), t3.at[j, 0], b_dn)
            receive((j, "rb-"), t3.at[j, 1], b_up)
            receive((j, "rb2"), t3.at[j, 2], b_far)
            diag_out[0, :, cols] = r2[j, pb] + t3[j, 0] + t3[j, 1] + t3[j, 2]

        return step_0, step_1, step_2, step_3, step_4

    sums = [sum_steps(j) for j in (2, 1, 0)]
    sums[0][0]()
    sums[1][0]()
    add_chips(stream_b, low_b, acc_b, first_five + next_six)
    sums[0][1]()
    sums[1][1]()
    settle(mark_3)
    group_4(stream_b)
    add_chips(stream_b, low_b, acc_b, last_five)
    sums[2][0]()
    store_rows = pltpu.make_async_copy(rows_buf, rows_out.at[0], local_sems.at[0])
    store_rows.start()
    for piece, step in ((0, 2), (2, 1), (1, 2), (0, 3), (2, 2), (1, 3), (0, 4), (2, 3), (1, 4), (2, 4)):
        sums[piece][step]()
    settle(len(started))
    store_rows.wait()


def negate(rows_ref, diag_ref, rows_out, diag_out):
    rows_out[...] = -rows_ref[...]
    diag_out[...] = diag_ref[...]


def shards(ancestor_inv, lower_block, diag_inverse, row_index):
    any_spec = pl.BlockSpec(memory_space=pl.ANY)
    vmem = pltpu.VMEM
    count = 224
    rows, diag = pl.pallas_call(
        body,
        out_shape=(jax.ShapeDtypeStruct((1, ROWS_L, 768), F32), jax.ShapeDtypeStruct((1, ROWS_D, 768), F32)),
        in_specs=[any_spec] * 4,
        out_specs=(any_spec, pl.BlockSpec(memory_space=pltpu.VMEM)),
        scratch_shapes=[
            vmem((192, 3072), F32),
            vmem((1, 3840), jnp.int32),
            vmem((1, 3840), jnp.int32),
            vmem((16, PAIR), jnp.int32),
            vmem((16, PAIR), jnp.int32),
            vmem((PAIR, 3072), BF16),
            vmem((8, ROWS_L, PAIR), F32),
            vmem((8, ROWS_L, PAIR), F32),
            vmem((16, 2 * PAD, PAIR), BF16),
            vmem((16, PAIR, 2 * W), F32),
            vmem((16, PAIR, W), F32),
            vmem((PAD, 2 * W), F32),
            vmem((PAD, W), F32),
            vmem((32, 3 * ROWS_D, W), F32),
            vmem((768, 768), BF16),
            vmem((768, 768), BF16),
            vmem((768, ROWS_L + ROWS_D), BF16),
            vmem((768, ROWS_L + ROWS_D), BF16),
            vmem((3, 16, 2, ROWS_D, W), F32),
            vmem((3, 16, ROWS_D, W), F32),
            vmem((3, 4, 4, ROWS_D, W), F32),
            vmem((3, 2, 2, ROWS_D, W), F32),
            vmem((3, 2, 4, ROWS_D, W), F32),
            vmem((3, 4, ROWS_D, W), F32),
            vmem((3, 3, ROWS_D, W), F32),
            vmem((ROWS_L, 768), F32),
            pltpu.SemaphoreType.DMA((8,)),
            pltpu.SemaphoreType.DMA((count,)),
            pltpu.SemaphoreType.DMA((count,)),
        ],
        compiler_params=pltpu.CompilerParams(
            collective_id=0, has_side_effects=True, vmem_limit_bytes=58 * 1024 * 1024),
    )(ancestor_inv, lower_block, diag_inverse, row_index)
    return pl.pallas_call(
        negate,
        out_shape=(jax.ShapeDtypeStruct(rows.shape, F32), jax.ShapeDtypeStruct(diag.shape, F32)),
    )(rows, diag)


def solution(mesh):
    in_specs = (P("grp", "blk", None), P("grp", "blk", None), P("grp", "blk", None), P("grp", None))
    out_specs = (P("grp", "blk", None), P("grp", "blk", None))
    return jax.shard_map(shards, mesh=mesh, in_specs=in_specs, out_specs=out_specs, check_vma=False)
```
